32 devices in a mesh: dp: 4 (over x, core), fsdp: 8 (over z, y).
Axes of the slice: x: 2, y: 2, z: 4, core: 2. Of those that a mesh axis runs over, the one named last changes fastest.
Arguments:
- tokens: bfloat16 [65536, 1024], P(('dp', 'fsdp')), may hold values from -6 to 6
- cotangent: bfloat16 [65536, 1024], P(('dp', 'fsdp')), may hold values from -6 to 6
- doc_lengths: int32 [32], P(('dp', 'fsdp')), may hold values from 896 to 2048, as said below
- key_keep: int32 [65536], P(('dp', 'fsdp')), may hold values 0 or 1
- random_blocks: int32 [1024, 16, 3], P(('dp', 'fsdp')), may hold values from 0 to 31
- attention_gain: bfloat16 [1024], P(('dp', 'fsdp')), may hold values from 0.5 to 1.5
- attention_shift: bfloat16 [1024], P(('dp', 'fsdp')), may hold values from -3 to 3
- w_query: bfloat16 [1024, 1024], P(('dp', 'fsdp')), may hold values from -0.1875 to 0.1875
- b_query: bfloat16 [1024], P(('dp', 'fsdp')), may hold values from -3 to 3
- w_key: bfloat16 [1024, 1024], P(('dp', 'fsdp')), may hold values from -0.1875 to 0.1875
- w_value: bfloat16 [1024, 1024], P(('dp', 'fsdp')), may hold values from -0.1875 to 0.1875
- b_value: bfloat16 [1024], P(('dp', 'fsdp')), may hold values from -3 to 3
- w_output: bfloat16 [1024, 1024], P(('dp', 'fsdp')), may hold values from -4 to 4
- b_output: bfloat16 [1024], P(('dp', 'fsdp')), may hold values from -3 to 3
- dense_gain: bfloat16 [1024], P(('dp', 'fsdp')), may hold values from 0.5 to 1.5
- dense_shift: bfloat16 [1024], P(('dp', 'fsdp')), may hold values from -3 to 3
- w_inner: bfloat16 [1024, 4096], P(('dp', 'fsdp')), may hold values from -0.1875 to 0.1875
- b_inner: bfloat16 [4096], P(('dp', 'fsdp')), may hold values from -3 to 3
- w_outer: bfloat16 [4096, 1024], P(('dp', 'fsdp')), may hold values from -0.09375 to 0.09375
- b_outer: bfloat16 [1024], P(('dp', 'fsdp')), may hold values from -3 to 3
Outputs:
- layer_output: bfloat16 [65536, 1024], P(('dp', 'fsdp'))
- input_grad: float32 [65536, 1024], P(('dp', 'fsdp'))
- attention_gain_grad: float32 [1024], P(('dp', 'fsdp'))
- attention_shift_grad: float32 [1024], P(('dp', 'fsdp'))
- w_query_grad: float32 [1024, 1024], P(('dp', 'fsdp'))
- b_query_grad: float32 [1024], P(('dp', 'fsdp'))
- w_key_grad: float32 [1024, 1024], P(('dp', 'fsdp'))
- w_value_grad: float32 [1024, 1024], P(('dp', 'fsdp'))
- b_value_grad: float32 [1024], P(('dp', 'fsdp'))
- w_output_grad: float32 [1024, 1024], P(('dp', 'fsdp'))
- b_output_grad: float32 [1024], P(('dp', 'fsdp'))
- dense_gain_grad: float32 [1024], P(('dp', 'fsdp'))
- dense_shift_grad: float32 [1024], P(('dp', 'fsdp'))
- w_inner_grad: float32 [1024, 4096], P(('dp', 'fsdp'))
- b_inner_grad: float32 [4096], P(('dp', 'fsdp'))
- w_outer_grad: float32 [4096, 1024], P(('dp', 'fsdp'))
- b_outer_grad: float32 [1024], P(('dp', 'fsdp'))
The draws below stay inside these ranges and needn't reach their ends.
Inputs may be any that keep to these rules, and one draw needn't show every extreme that they name: `doc_lengths`: each document's length in tokens; some document has exactly 2048 tokens in every draw, and most have about half of that.
All inputs are finite; a program needn't handle non-finite values. No bound on the sum of `key_keep` on one device may be relied on, other than what follows from the above.
Results may differ from the reference program's by a relative error of at most 0.012.
Values may be sent and summed in bfloat16 or wider, within the bound.
No kernel may reach another device: no remote copies, remote signals or barrier semaphores. Data moves between devices by JAX's collectives and lax.ppermute only.
A program may use at most 576 MiB of HBM per device.

```python
import jax
import jax.numpy as jnp
from jax import lax

D = 1024
HEADS = 16
HEAD = 64
FF = 4096
BLOCK = 64
RANDOM = 3
WINDOW = 3
GLOBAL = 2
TOK_DEV = 2048
DOCS = 32
TOKENS = 65536


def draw_doc_lengths(key, part):
    first, second, third, fourth = jax.random.split(key, 4)
    shorter = jax.random.randint(first, (DOCS,), TOK_DEV // 2 - 2 * BLOCK, TOK_DEV // 2 + 1)
    longer = jax.random.randint(second, (DOCS,), TOK_DEV - 2 * BLOCK, TOK_DEV + 1)
    chosen = jax.random.randint(third, (DOCS,), 0, 8) == 0
    lengths = jnp.where(chosen, longer, shorter)
    fullest = jax.random.randint(fourth, (), 0, DOCS)
    return lengths.at[fullest].set(TOK_DEV).astype(jnp.int32)


def touch_ends(values, key, low, high):
    place = [jax.random.randint(jax.random.fold_in(key, axis), (), 0, length) for axis, length in enumerate(values.shape)]
    main_axis = values.shape.index(max(values.shape))
    neighbour = place[:main_axis] + [(place[main_axis] + 1) % values.shape[main_axis]] + place[main_axis + 1:]
    return values.at[tuple(place)].set(low).at[tuple(neighbour)].set(high)


def raised(entries, stream_key, source, target, blocks, factor):
    owner, partner = [(jnp.arange(entries.shape[dim]) // (entries.shape[dim] // blocks)).reshape([-1 if axis == dim else 1 for axis in range(entries.ndim)]) for dim in (source, target)]
    chosen = jax.random.permutation(stream_key, blocks)[partner]
    strong = (owner == chosen) | (owner == (partner + blocks // 2) % blocks)
    return jnp.where(strong, factor * entries, entries)


def level_of(rng, extent, cuts, least, top_value):
    level, own = 1.0, jax.random.fold_in(rng, 6)
    for dim, parts in cuts:
        heights = jnp.exp(jax.random.uniform(jax.random.fold_in(own, dim), (parts,), jnp.float32, least / len(cuts), top_value / len(cuts)))
        level = level * jnp.repeat(heights, extent[dim] // parts).reshape([-1 if axis == dim else 1 for axis in range(len(extent))])
    return level


def gaussian(own_key, extent, scale, reach, cuts=(), kind=jnp.bfloat16):
    array = jax.random.normal(own_key, extent, jnp.float32) * scale
    if len(cuts) > 0:
        array = level_of(own_key, extent, cuts, -0.22, 0.18) * array
    return jnp.clip(array, min=-reach, max=reach).astype(kind)


def noise_with(key, shape, scale, reach, cuts, heavy, kind=jnp.bfloat16):
    array = scale * jax.random.normal(key, shape, jnp.float32)
    if cuts:
        array = array * level_of(key, shape, cuts, -0.22, 0.18)
    return jnp.clip(raised(array, jax.random.fold_in(key, 3), *heavy), -reach, reach).astype(kind)


def setup_inputs(seed: int = 0) -> dict:
    key_list = jax.random.split(jax.random.key(seed), 21)
    return {
        "tokens": gaussian(key_list[0], (TOKENS, D), 1.0, 6.0, ((0, 32),)),
        "cotangent": noise_with(key_list[1], (TOKENS, D), 1.0, 6.0, ((0, 32),), (0, 1, 32, 2.75)),
        "doc_lengths": draw_doc_lengths(jax.random.fold_in(key_list[20], 71), 0),
        "key_keep": touch_ends((jax.random.randint(key_list[3], (TOKENS,), 0, 16) < 15).astype(jnp.int32), jax.random.fold_in(key_list[3], 1), 0, 1),
        "random_blocks": touch_ends(jax.random.randint(key_list[4], (TOKENS // BLOCK, HEADS, RANDOM), 0, TOK_DEV // BLOCK), jax.random.fold_in(key_list[4], 1), 0, (TOK_DEV // BLOCK) - 1).astype(jnp.int32),
        "attention_gain": jnp.clip(1.0 + 0.1 * jax.random.normal(key_list[5], (D,), jnp.float32), 0.5, 1.5).astype(jnp.bfloat16),
        "attention_shift": gaussian(key_list[6], (D,), 0.5, 3.0, ((0, 32),)),
        "w_query": gaussian(key_list[7], (D, D), D ** -0.5, 0.1875, ((0, 32),)),
        "b_query": gaussian(key_list[8], (D,), 0.5, 3.0, ((0, 32),)),
        "w_key": gaussian(key_list[9], (D, D), D ** -0.5, 0.1875, ((0, 32),)),
        "w_value": gaussian(key_list[10], (D, D), D ** -0.5, 0.1875, ((0, 32),)),
        "b_value": gaussian(key_list[11], (D,), 0.5, 3.0, ((0, 32),)),
        "w_output": gaussian(key_list[12], (D, D), (max(1, D // ((WINDOW + RANDOM + GLOBAL) * BLOCK))) ** -0.5, 4.0, ((0, 32),)),
        "b_output": gaussian(key_list[13], (D,), 0.5, 3.0, ((0, 32),)),
        "dense_gain": jnp.clip(1.0 + 0.1 * jax.random.normal(key_list[14], (D,), jnp.float32), 0.5, 1.5).astype(jnp.bfloat16),
        "dense_shift": gaussian(key_list[15], (D,), 0.5, 3.0, ((0, 32),)),
        "w_inner": gaussian(key_list[16], (D, FF), D ** -0.5, 0.1875, ((0, 32),)),
        "b_inner": gaussian(key_list[17], (FF,), 0.5, 3.0, ((0, 32),)),
        "w_outer": gaussian(key_list[18], (FF, D), FF ** -0.5, 0.09375, ((0, 32),)),
        "b_outer": gaussian(key_list[19], (D,), 0.5, 3.0, ((0, 32),)),
    }


EPSILON = 1e-05
NEGATIVE = -1e+30
PRECISE = lax.Precision.HIGHEST

@jax.custom_vjp
def low(v):
    return lax.optimization_barrier(v.astype(jnp.bfloat16)).astype(jnp.float32)

@jax.custom_vjp
def low_back(v):
    return v

def low_keep(v):
    return (low(v), None)

def low_pass(kept, grad):
    return (grad,)

def back_keep(v):
    return (v, None)

def back_low(kept, grad):
    return (low(grad),)
low.defvjp(low_keep, low_pass)
low_back.defvjp(back_keep, back_low)

def rounded_both(values_in):
    return low(low_back(values_in))

def norm_rows(values_in, norm_gain, norm_shift):
    centre = values_in - lax.optimization_barrier(jnp.mean(values_in, -1, keepdims=True))
    spread = lax.optimization_barrier(jnp.mean(centre * centre, -1, keepdims=True))
    return centre * lax.rsqrt(spread + EPSILON) * norm_gain + norm_shift

def block_table(random_doc, block_count):
    margin = WINDOW // 2
    blocks = jnp.arange(block_count, dtype=jnp.int32)
    nearby = blocks[:, None] + jnp.arange(WINDOW, dtype=jnp.int32)[None, :]
    nearby = jnp.broadcast_to(nearby[None], (HEADS, block_count, WINDOW))
    distant = jnp.transpose(random_doc, (1, 0, 2)).astype(jnp.int32) + margin
    leading = jnp.arange(GLOBAL, dtype=jnp.int32) + margin
    leading = jnp.broadcast_to(leading, (HEADS, block_count, GLOBAL))
    return jnp.concatenate([nearby, distant, leading], -1).astype(jnp.int32)

def pick_blocks(padded, block_index):
    return jax.vmap(lambda source, chosen: source[chosen])(padded, block_index)

def attention(queries, key_rows, value_rows, live_keys, random_doc):
    length = queries.shape[0]
    block_count = length // BLOCK
    margin = WINDOW // 2

    def split_pad(flat_rows):
        blocked = flat_rows.reshape(block_count, BLOCK, HEADS, HEAD).transpose(2, 0, 1, 3)
        return jnp.pad(blocked, ((0, 0), (margin, margin), (0, 0), (0, 0)))
    query_split = queries.reshape(block_count, BLOCK, HEADS, HEAD).transpose(2, 0, 1, 3)
    key_pad = split_pad(key_rows)
    value_pad = split_pad(value_rows)
    live_pad = jnp.pad(live_keys.reshape(block_count, BLOCK), ((margin, margin), (0, 0)))
    block_index = block_table(random_doc, block_count)
    listed = block_index.shape[-1] * BLOCK
    key_picked = pick_blocks(key_pad, block_index).reshape(HEADS, block_count, listed, HEAD)
    value_picked = pick_blocks(value_pad, block_index).reshape(HEADS, block_count, listed, HEAD)
    live_picked = live_pad[block_index].reshape(HEADS, block_count, 1, listed)
    scores = low_back(jnp.einsum('hnqd,hnkd->hnqk', query_split, key_picked, precision=PRECISE))
    scores = jnp.where(live_picked, scores, NEGATIVE)
    local_weights = low(jax.nn.softmax(scores, -1))
    local_out = jnp.einsum('hnqk,hnkd->hnqd', local_weights, value_picked, precision=PRECISE)
    lead_rows = query_split[:, :GLOBAL].reshape(HEADS, GLOBAL * BLOCK, HEAD)
    key_all = key_rows.reshape(length, HEADS, HEAD).transpose(1, 0, 2)
    value_all = value_rows.reshape(length, HEADS, HEAD).transpose(1, 0, 2)
    lead_scores = low_back(jnp.einsum('hqd,hkd->hqk', lead_rows, key_all, precision=PRECISE))
    lead_scores = jnp.where(live_keys[None, None, :], lead_scores, NEGATIVE)
    lead_weights = low(jax.nn.softmax(lead_scores, -1))
    lead_out = jnp.einsum('hqk,hkd->hqd', lead_weights, value_all, precision=PRECISE)
    merged = jnp.concatenate([lead_out.reshape(HEADS, GLOBAL, BLOCK, HEAD), local_out[:, GLOBAL:]], 1)
    return merged.transpose(1, 2, 0, 3).reshape(length, HEADS * HEAD)

def layer(inputs, live_keys, random_doc, params):
    attention_gain, attention_shift, w_query, b_query, w_key, w_value, b_value, w_output, b_output, dense_gain, dense_shift, w_inner, b_inner, w_outer, b_outer = params
    scaling = HEAD ** (-0.5)
    normed = low(norm_rows(inputs, attention_gain, attention_shift))
    queries = rounded_both((jnp.dot(normed, w_query, precision=PRECISE) + b_query) * scaling)
    key_rows = rounded_both(jnp.dot(normed, w_key, precision=PRECISE))
    value_rows = rounded_both(jnp.dot(normed, w_value, precision=PRECISE) + b_value)
    mixture = rounded_both(attention(queries, key_rows, value_rows, live_keys, random_doc))
    branch = low_back(jnp.dot(mixture, w_output, precision=PRECISE) + b_output)
    residual = inputs + branch
    dense_normed = low(norm_rows(residual, dense_gain, dense_shift))
    hidden = low_back(jnp.dot(dense_normed, w_inner, precision=PRECISE) + b_inner)
    active = low(jax.nn.gelu(hidden, approximate=True))
    return residual + low_back(jnp.dot(active, w_outer, precision=PRECISE) + b_outer)

def reference(tokens, cotangent, doc_lengths, key_keep, random_blocks, attention_gain, attention_shift, w_query, b_query, w_key, w_value, b_value, w_output, b_output, dense_gain, dense_shift, w_inner, b_inner, w_outer, b_outer):
    params = jax.tree.map(lambda weight: weight.astype(jnp.float32), (attention_gain, attention_shift, w_query, b_query, w_key, w_value, b_value, w_output, b_output, dense_gain, dense_shift, w_inner, b_inner, w_outer, b_outer))
    block_count = TOK_DEV // BLOCK
    places = jnp.arange(TOK_DEV, dtype=jnp.int32)
    inputs_all = tokens.astype(jnp.float32).reshape(DOCS, TOK_DEV, D)
    grads_all = cotangent.astype(jnp.float32).reshape(DOCS, TOK_DEV, D)
    live_all = (key_keep.reshape(DOCS, TOK_DEV) > 0) & (places[None, :] < doc_lengths[:, None]) | (places[None, :] == 0)
    random_all = random_blocks.reshape(DOCS, block_count, HEADS, RANDOM)

    def one_document(totals, document):
        inputs, grad_rows, live_keys, random_doc = document
        output, pullback = jax.vjp(lambda first, second: layer(first, live_keys, random_doc, second), inputs, params)
        input_grad, param_grads = pullback(grad_rows)
        return (jax.tree.map(jnp.add, totals, param_grads), (output.astype(jnp.bfloat16), input_grad))
    starting = jax.tree.map(jnp.zeros_like, params)
    totals, (outputs, input_grads) = lax.scan(one_document, starting, (inputs_all, grads_all, live_all, random_all))
    return (outputs.reshape(TOKENS, D), input_grads.reshape(TOKENS, D), totals[0], totals[1], totals[2], totals[3], totals[4], totals[5], totals[6], totals[7], totals[8], totals[9], totals[10], totals[11], totals[12], totals[13], totals[14])
```

```python
import jax
import jax.numpy as jnp
from jax import lax
from jax.experimental import pallas as pl
from jax.experimental.pallas import tpu as pltpu

HEADS = 16
HEAD = 64
BLOCK = 64
RANDOM = 3
GLOBAL = 2
NEGATIVE = -1e30
GROUP = 4
WIDE = GROUP * HEAD
LISTED = 8 * BLOCK
CHUNK = 512
SCALING = HEAD ** (-0.5)


def dot_nt(left, right):
    return lax.dot_general(left, right, (((1,), (1,)), ((), ())), preferred_element_type=jnp.float32)


def dot_nn(left, right):
    return lax.dot_general(left, right, (((1,), (0,)), ((), ())), preferred_element_type=jnp.float32)


def dot_tn(left, right):
    return lax.dot_general(left, right, (((0,), (0,)), ((), ())), preferred_element_type=jnp.float32)


def spread_heads(rows, same_head):
    return jnp.concatenate([rows] * GROUP, 0) * same_head


def own_lanes(full):
    lane_head = lax.broadcasted_iota(jnp.int32, (BLOCK, WIDE), 1) // HEAD
    picked = full[:BLOCK]
    for head in range(1, GROUP):
        picked = jnp.where(lane_head == head, full[head * BLOCK : (head + 1) * BLOCK], picked)
    return picked


def rows_of(block):
    return pl.ds(pl.multiple_of(block * BLOCK, BLOCK), BLOCK)


def chosen(table_ref, row, first_head):
    base = (row * HEADS + first_head) * RANDOM
    return [[table_ref[base + head * RANDOM + pick] for head in range(GROUP)] for pick in range(RANDOM)]


def paired(ref, numbers, low_half, whole):
    parts = []
    for pair in range(GROUP // 2):
        lanes = slice(pair * 128, (pair + 1) * 128) if whole else slice(0, 128)
        first = ref[rows_of(numbers[2 * pair]), lanes]
        second = ref[rows_of(numbers[2 * pair + 1]), lanes]
        parts.append(jnp.where(low_half, first, second))
    return jnp.concatenate(parts, 1)


def listed_rows(ref, row, after, picks, low_half):
    parts = [ref[rows_of(row - 1), :], ref[rows_of(row), :], ref[rows_of(after), :]]
    parts += [paired(ref, numbers, low_half, True) for numbers in picks]
    parts.append(ref[: GLOBAL * BLOCK, :])
    return jnp.concatenate(parts, 0)


def listed_bias(bias_ref, row, picks, low_half):
    def twice(value):
        return jnp.concatenate([value] * (GROUP // 2), 1)

    parts = [twice(bias_ref[rows_of(row - 1), :]), twice(bias_ref[rows_of(row), :])]
    parts.append(twice(bias_ref[rows_of(row + 1), :]))
    parts += [paired(bias_ref, numbers, low_half, False) for numbers in picks]
    parts.append(twice(bias_ref[: GLOBAL * BLOCK, :]))
    return jnp.concatenate(parts, 0)


def lane_masks():
    low_half = lax.broadcasted_iota(jnp.int32, (BLOCK, 128), 1) < HEAD
    one = lax.broadcasted_iota(jnp.int32, (WIDE, WIDE), 0) // HEAD
    two = lax.broadcasted_iota(jnp.int32, (WIDE, WIDE), 1) // HEAD
    same_head = jnp.where(one == two, 1.0, 0.0).astype(jnp.bfloat16)
    return low_half, same_head


def forward_kernel(table_ref, q_ref, k_ref, v_ref, bias_ref, out_ref, lse_ref, score_ref):
    length = q_ref.shape[0]
    block_count = length // BLOCK
    first_head = pl.program_id(0) * GROUP
    low_half, same_head = lane_masks()

    def local_row(row, carried):
        picks = chosen(table_ref, row, first_head)
        after = jnp.minimum(row + 1, block_count - 1)
        query = spread_heads(q_ref[rows_of(row), :], same_head)
        keys = listed_rows(k_ref, row, after, picks, low_half)
        scores = dot_nt(keys, query) + listed_bias(bias_ref, row, picks, low_half)
        highest = jnp.max(scores, 0, keepdims=True)
        expanded = jnp.exp(scores - highest)
        total = jnp.sum(expanded, 0, keepdims=True)
        weights = (expanded * (1.0 / total)).astype(jnp.bfloat16)
        values = listed_rows(v_ref, row, after, picks, low_half)
        out_ref[rows_of(row), :] = own_lanes(dot_tn(weights, values)).astype(jnp.bfloat16)
        lse_ref[0, pl.ds(row, 1), :] = highest + jnp.log(total)
        return carried

    for row in range(GLOBAL):
        query = spread_heads(q_ref[row * BLOCK : (row + 1) * BLOCK, :], same_head)

        def score_chunk(chunk, highest):
            span = pl.ds(pl.multiple_of(chunk * CHUNK, CHUNK), CHUNK)
            bias = bias_ref[span, :]
            scores = dot_nt(k_ref[span, :], query) + jnp.concatenate([bias] * (GROUP // 2), 1)
            score_ref[span, :] = scores
            return jnp.maximum(highest, jnp.max(scores, 0, keepdims=True))

        highest = lax.fori_loop(
            0, length // CHUNK, score_chunk, jnp.full((1, WIDE), NEGATIVE, jnp.float32)
        )

        def total_chunk(chunk, total):
            span = pl.ds(pl.multiple_of(chunk * CHUNK, CHUNK), CHUNK)
            expanded = jnp.exp(score_ref[span, :] - highest)
            score_ref[span, :] = expanded
            return total + jnp.sum(expanded, 0, keepdims=True)

        total = lax.fori_loop(
            0, length // CHUNK, total_chunk, jnp.zeros((1, WIDE), jnp.float32)
        )
        inverse = 1.0 / total

        def mix_chunk(chunk, mixed):
            span = pl.ds(pl.multiple_of(chunk * CHUNK, CHUNK), CHUNK)
            weights = (score_ref[span, :] * inverse).astype(jnp.bfloat16)
            return mixed + own_lanes(dot_tn(weights, v_ref[span, :]))

        mixed = lax.fori_loop(
            0, length // CHUNK, mix_chunk, jnp.zeros((BLOCK, WIDE), jnp.float32)
        )
        out_ref[row * BLOCK : (row + 1) * BLOCK, :] = mixed.astype(jnp.bfloat16)
        lse_ref[0, row : row + 1, :] = highest + jnp.log(total)

    lax.fori_loop(GLOBAL, block_count, local_row, 0)


def backward_kernel(
    table_ref,
    q_ref,
    k_ref,
    v_ref,
    grad_ref,
    bias_ref,
    lse_ref,
    dq_ref,
    dk_ref,
    dv_ref,
    chance_ref,
    pull_ref,
    dk_sum,
    dv_sum,
):
    length = q_ref.shape[0]
    block_count = length // BLOCK
    first_head = pl.program_id(0) * GROUP
    low_half, same_head = lane_masks()

    for row in range(GLOBAL):
        query = spread_heads(q_ref[row * BLOCK : (row + 1) * BLOCK, :], same_head)
        grad = spread_heads(grad_ref[row * BLOCK : (row + 1) * BLOCK, :], same_head)
        lse = lse_ref[0, row : row + 1, :]

        def chance_chunk(chunk, centred):
            span = pl.ds(pl.multiple_of(chunk * CHUNK, CHUNK), CHUNK)
            bias = bias_ref[span, :]
            scores = dot_nt(k_ref[span, :], query) + jnp.concatenate([bias] * (GROUP // 2), 1)
            chances = jnp.exp(scores - lse)
            pulls = dot_nt(v_ref[span, :], grad)
            chance_ref[span, :] = chances
            pull_ref[span, :] = pulls
            return centred + jnp.sum(chances * pulls, 0, keepdims=True)

        centred = lax.fori_loop(
            0, length // CHUNK, chance_chunk, jnp.zeros((1, WIDE), jnp.float32)
        )

        def grad_chunk(chunk, query_grad):
            span = pl.ds(pl.multiple_of(chunk * CHUNK, CHUNK), CHUNK)
            chances = chance_ref[span, :]
            score_grad = (chances * (pull_ref[span, :] - centred)).astype(jnp.bfloat16)
            key_part = dot_nn(score_grad, query)
            value_part = dot_nn(chances.astype(jnp.bfloat16), grad)
            if row == 0:
                dk_sum[span, :] = key_part
                dv_sum[span, :] = value_part
            else:
                dk_sum[span, :] += key_part
                dv_sum[span, :] += value_part
            return query_grad + own_lanes(dot_tn(score_grad, k_ref[span, :]))

        query_grad = lax.fori_loop(
            0, length // CHUNK, grad_chunk, jnp.zeros((BLOCK, WIDE), jnp.float32)
        )
        dq_ref[row * BLOCK : (row + 1) * BLOCK, :] = (query_grad * SCALING).astype(jnp.bfloat16)

    dk_sum[length : length + BLOCK, :] = jnp.zeros((BLOCK, WIDE), jnp.float32)
    dv_sum[length : length + BLOCK, :] = jnp.zeros((BLOCK, WIDE), jnp.float32)

    def add_rows(sum_ref, part, row, picks):
        near = pl.ds(pl.multiple_of((row - 1) * BLOCK, BLOCK), 3 * BLOCK)
        sum_ref[near, :] += part[: 3 * BLOCK]
        for pick, numbers in enumerate(picks):
            piece = part[(3 + pick) * BLOCK : (4 + pick) * BLOCK]
            for head, number in enumerate(numbers):
                lanes = slice(head // 2 * 128, (head // 2 + 1) * 128)
                mine = low_half if head % 2 == 0 else jnp.logical_not(low_half)
                sum_ref[rows_of(number), lanes] += jnp.where(mine, piece[:, lanes], 0.0)
        sum_ref[: GLOBAL * BLOCK, :] += part[6 * BLOCK :]

    def local_row(row, carried):
        picks = chosen(table_ref, row, first_head)
        after = jnp.minimum(row + 1, block_count - 1)
        query = spread_heads(q_ref[rows_of(row), :], same_head)
        grad = spread_heads(grad_ref[rows_of(row), :], same_head)
        keys = listed_rows(k_ref, row, after, picks, low_half)
        values = listed_rows(v_ref, row, after, picks, low_half)
        scores = dot_nt(keys, query) + listed_bias(bias_ref, row, picks, low_half)
        chances = jnp.exp(scores - lse_ref[0, pl.ds(row, 1), :])
        pulls = dot_nt(values, grad)
        centred = jnp.sum(chances * pulls, 0, keepdims=True)
        score_grad = (chances * (pulls - centred)).astype(jnp.bfloat16)
        query_grad = own_lanes(dot_tn(score_grad, keys))
        dq_ref[rows_of(row), :] = (query_grad * SCALING).astype(jnp.bfloat16)
        add_rows(dk_sum, dot_nn(score_grad, query), row, picks)
        add_rows(dv_sum, dot_nn(chances.astype(jnp.bfloat16), grad), row, picks)
        return carried

    lax.fori_loop(GLOBAL, block_count, local_row, 0)
    dk_ref[...] = dk_sum[:length, :].astype(jnp.bfloat16)
    dv_ref[...] = dv_sum[:length, :].astype(jnp.bfloat16)


def attention_specs(length, count):
    rows = pl.BlockSpec((length, WIDE), lambda group, table: (0, group))
    bias = pl.BlockSpec((length + BLOCK, 128), lambda group, table: (0, 0))
    lse = pl.BlockSpec((1, length // BLOCK, WIDE), lambda group, table: (group, 0, 0))
    return [rows] * count, bias, lse


def live_bias(live_keys):
    padded = jnp.concatenate([live_keys, jnp.zeros((BLOCK,), jnp.bool_)])
    return jnp.broadcast_to(jnp.where(padded, 0.0, NEGATIVE)[:, None], (padded.shape[0], 128))


def attention_forward(queries, key_rows, value_rows, bias, table):
    length, width = queries.shape
    rows, bias_spec, lse_spec = attention_specs(length, 3)
    units = width // WIDE * (length // BLOCK + 6)
    return pl.pallas_call(
        forward_kernel,
        grid_spec=pltpu.PrefetchScalarGridSpec(
            num_scalar_prefetch=1,
            grid=(width // WIDE,),
            in_specs=rows + [bias_spec],
            out_specs=[rows[0], lse_spec],
            scratch_shapes=[pltpu.VMEM((length, WIDE), jnp.float32)],
        ),
        out_shape=[
            jax.ShapeDtypeStruct((length, width), jnp.bfloat16),
            jax.ShapeDtypeStruct((width // WIDE, length // BLOCK, WIDE), jnp.float32),
        ],
        cost_estimate=pl.CostEstimate(
            flops=units * 4 * LISTED * WIDE * WIDE,
            bytes_accessed=8 * length * width,
            transcendentals=units * LISTED * WIDE,
        ),
        compiler_params=pltpu.CompilerParams(vmem_limit_bytes=48 << 20),
        name="block_attention",
    )(table, queries, key_rows, value_rows, bias)


def attention_backward(queries, key_rows, value_rows, bias, table, lse, mixture_grad):
    length, width = queries.shape
    rows, bias_spec, lse_spec = attention_specs(length, 4)
    units = width // WIDE * (length // BLOCK + 6)
    return pl.pallas_call(
        backward_kernel,
        grid_spec=pltpu.PrefetchScalarGridSpec(
            num_scalar_prefetch=1,
            grid=(width // WIDE,),
            in_specs=rows + [bias_spec, lse_spec],
            out_specs=[rows[0]] * 3,
            scratch_shapes=[
                pltpu.VMEM((length, WIDE), jnp.float32),
                pltpu.VMEM((length, WIDE), jnp.float32),
                pltpu.VMEM((length + BLOCK, WIDE), jnp.float32),
                pltpu.VMEM((length + BLOCK, WIDE), jnp.float32),
            ],
        ),
        out_shape=[jax.ShapeDtypeStruct((length, width), jnp.bfloat16)] * 3,
        cost_estimate=pl.CostEstimate(
            flops=units * 10 * LISTED * WIDE * WIDE,
            bytes_accessed=14 * length * width,
            transcendentals=units * LISTED * WIDE,
        ),
        compiler_params=pltpu.CompilerParams(vmem_limit_bytes=56 << 20),
        name="block_attention_grad",
    )(table, queries, key_rows, value_rows, mixture_grad, bias, lse)


from jax.sharding import PartitionSpec as P

EPSILON = 1e-05
SPLIT = ("dp", "fsdp")


def norm_rows(values_in, norm_gain, norm_shift):
    centre = values_in - jnp.mean(values_in, -1, keepdims=True)
    inverse = lax.rsqrt(jnp.mean(centre * centre, -1, keepdims=True) + EPSILON)
    unit_rows = centre * inverse
    return (unit_rows * norm_gain + norm_shift, unit_rows, inverse)


def norm_back(grad_rows, unit_rows, inverse, norm_gain):
    scaled = grad_rows * norm_gain
    adjusted = (
        scaled
        - jnp.mean(scaled, -1, keepdims=True)
        - unit_rows * jnp.mean(scaled * unit_rows, -1, keepdims=True)
    )
    return (adjusted * inverse, jnp.sum(grad_rows * unit_rows, 0), jnp.sum(grad_rows, 0))


def product(left, right):
    return jnp.dot(left, right, preferred_element_type=jnp.float32)


def across_rows(left, right):
    return jnp.einsum("ti,tj->ij", left, right, preferred_element_type=jnp.float32)


def against(left, right):
    return jnp.einsum("ti,ji->tj", left, right, preferred_element_type=jnp.float32)


class Grid:
    def __init__(self, mesh):
        self.bits = []
        self.size = {}
        for name in SPLIT:
            count = mesh.shape[name]
            self.size[name] = count
            for bit in reversed(range(count.bit_length() - 1)):
                self.bits.append((name, bit))

    def mine(self, place):
        name, bit = self.bits[place]
        return (lax.axis_index(name) >> bit) & 1

    def swap(self, values_in, place):
        name, bit = self.bits[place]
        pairs = [(source, source ^ (1 << bit)) for source in range(self.size[name])]
        return lax.ppermute(values_in, name, pairs)

    def order(self, turn):
        chip = [place for place, (name, bit) in enumerate(self.bits) if name == "dp" and bit == 0]
        near = [place for place, (name, bit) in enumerate(self.bits) if name == "fsdp" and bit < 2]
        far = [place for place, (name, bit) in enumerate(self.bits) if name == "dp" and bit > 0]
        rest = [place for place in range(len(self.bits)) if place not in chip + near + far]
        ring = far + near
        turn = turn % max(1, len(ring))
        return chip + ring[turn:] + ring[:turn] + rest

    def scatter_sum(self, part, turn, low):
        total = part.reshape((2,) * len(self.bits) + (-1,) + part.shape[1:])
        left = list(range(len(self.bits)))
        for place in self.order(turn):
            dim = left.index(place)
            left.remove(place)
            mine = self.mine(place)
            given = lax.dynamic_index_in_dim(total, 1 - mine, dim, keepdims=False)
            kept = lax.dynamic_index_in_dim(total, mine, dim, keepdims=False)
            taken = self.swap(given.astype(low), place)
            total = kept.astype(jnp.float32) + taken.astype(jnp.float32)
        return total

    def gather(self, shard, turn):
        whole = shard
        have = []
        for place in reversed(self.order(turn)):
            taken = self.swap(whole, place)
            dim = sum(1 for other in have if other < place)
            have.append(place)
            first = self.mine(place) == 0
            whole = jnp.where(
                first, jnp.stack([whole, taken], dim), jnp.stack([taken, whole], dim)
            )
        return whole.reshape((-1,) + shard.shape[1:])


def solution(mesh):
    grid = Grid(mesh)

    def body(
        tokens,
        cotangent,
        doc_lengths,
        key_keep,
        random_blocks,
        attention_gain,
        attention_shift,
        w_query,
        b_query,
        w_key,
        w_value,
        b_value,
        w_output,
        b_output,
        dense_gain,
        dense_shift,
        w_inner,
        b_inner,
        w_outer,
        b_outer,
    ):
        vectors = (
            attention_gain,
            attention_shift,
            b_query,
            b_value,
            b_output,
            dense_gain,
            dense_shift,
            b_outer,
            b_inner,
        )
        share = attention_gain.shape[0]
        joined = grid.gather(jnp.concatenate(vectors)[None, :], 0).astype(jnp.float32)
        places = [share * number for number in range(9)]
        gain_one, shift_one, b_query, b_value, b_output, gain_two, shift_two, b_outer = [
            joined[:, start : start + share].reshape(-1) for start in places[:8]
        ]
        b_inner = joined[:, places[8] :].reshape(-1)
        w_query = grid.gather(w_query, 0)
        w_key = grid.gather(w_key, 1)
        w_value = grid.gather(w_value, 2)
        w_output = lax.all_gather(w_output, SPLIT, axis=0, tiled=True)
        w_inner = lax.all_gather(w_inner, SPLIT, axis=0, tiled=True)
        w_outer = lax.all_gather(w_outer, SPLIT, axis=0, tiled=True)

        scaling = HEAD ** (-0.5)
        length = tokens.shape[0]
        places = jnp.arange(length, dtype=jnp.int32)
        live_keys = (key_keep > 0) & (places < doc_lengths[0]) | (places == 0)
        bias = live_bias(live_keys)
        table = random_blocks.reshape(-1)
        inputs = tokens.astype(jnp.float32)
        normed_full, unit_one, inverse_one = norm_rows(inputs, gain_one, shift_one)
        normed = normed_full.astype(jnp.bfloat16)
        queries = ((product(normed, w_query) + b_query) * scaling).astype(jnp.bfloat16)
        key_rows = product(normed, w_key).astype(jnp.bfloat16)
        value_rows = (product(normed, w_value) + b_value).astype(jnp.bfloat16)
        mixture, lse = attention_forward(queries, key_rows, value_rows, bias, table)
        residual = inputs + (product(mixture, w_output) + b_output)
        dense_full, unit_two, inverse_two = norm_rows(residual, gain_two, shift_two)
        dense_low = dense_full.astype(jnp.bfloat16)
        hidden = product(dense_low, w_inner) + b_inner
        active_full, gelu_pull = jax.vjp(
            lambda pre_act: jax.nn.gelu(pre_act, approximate=True), hidden
        )
        active = active_full.astype(jnp.bfloat16)
        layer_output = (residual + (product(active, w_outer) + b_outer)).astype(jnp.bfloat16)

        grad_rows = cotangent.astype(jnp.float32)
        outer_weight_grad = grid.scatter_sum(across_rows(active, cotangent), 0, jnp.bfloat16)
        outer_bias_grad = jnp.sum(grad_rows, 0)
        hidden_grad = gelu_pull(against(cotangent, w_outer))[0].astype(jnp.bfloat16)
        inner_weight_grad = grid.scatter_sum(across_rows(dense_low, hidden_grad), 1, jnp.bfloat16)
        inner_bias_grad = jnp.sum(hidden_grad.astype(jnp.float32), 0)
        dense_normed_grad = against(hidden_grad, w_inner)
        residual_part, dense_gain_grad, dense_shift_grad = norm_back(
            dense_normed_grad, unit_two, inverse_two, gain_two
        )
        residual_grad = grad_rows + residual_part
        branch_grad = residual_grad.astype(jnp.bfloat16)
        output_weight_grad = grid.scatter_sum(across_rows(mixture, branch_grad), 2, jnp.bfloat16)
        output_bias_grad = jnp.sum(branch_grad.astype(jnp.float32), 0)
        mixture_grad = against(branch_grad, w_output).astype(jnp.bfloat16)
        query_low, key_low, value_low = attention_backward(
            queries, key_rows, value_rows, bias, table, lse, mixture_grad
        )
        query_weight_grad = grid.scatter_sum(across_rows(normed, query_low), 0, jnp.bfloat16)
        query_bias_grad = jnp.sum(query_low.astype(jnp.float32), 0)
        key_weight_grad = grid.scatter_sum(across_rows(normed, key_low), 1, jnp.bfloat16)
        value_weight_grad = grid.scatter_sum(across_rows(normed, value_low), 2, jnp.bfloat16)
        value_bias_grad = jnp.sum(value_low.astype(jnp.float32), 0)
        normed_grad = (
            against(query_low, w_query) + against(key_low, w_key) + against(value_low, w_value)
        )
        input_part, gain_one_grad, shift_one_grad = norm_back(
            normed_grad, unit_one, inverse_one, gain_one
        )
        input_grad = residual_grad + input_part

        def shares(vector):
            return vector.reshape(-1, share)

        grads = [
            gain_one_grad,
            shift_one_grad,
            query_bias_grad,
            value_bias_grad,
            output_bias_grad,
            dense_gain_grad,
            dense_shift_grad,
            outer_bias_grad,
        ]
        devices = gain_one_grad.shape[0] // share
        packed = jnp.concatenate(
            [shares(vector) for vector in grads] + [inner_bias_grad.reshape(devices, -1)], 1
        )
        vector_sums = grid.scatter_sum(packed, 0, jnp.float32).reshape(-1)
        sums = [vector_sums[start : start + share] for start in range(0, 8 * share, share)]
        return (
            layer_output,
            input_grad,
            sums[0],
            sums[1],
            query_weight_grad,
            sums[2],
            key_weight_grad,
            value_weight_grad,
            sums[3],
            output_weight_grad,
            sums[4],
            sums[5],
            sums[6],
            inner_weight_grad,
            vector_sums[8 * share :],
            outer_weight_grad,
            sums[7],
        )

    rows = P(SPLIT, None)
    flat = P(SPLIT)
    return jax.shard_map(
        body,
        mesh=mesh,
        in_specs=(
            (rows, rows, flat, flat, P(SPLIT, None, None), flat, flat, rows, flat, rows, rows)
            + (flat, rows, flat, flat, flat, rows, flat, rows, flat)
        ),
        out_specs=(
            (rows, rows, flat, flat, rows, flat, rows, rows, flat, rows, flat, flat, flat)
            + (rows, flat, rows, flat)
        ),
        check_vma=False,
    )
```

```python
import functools

import jax
import jax.numpy as jnp
from jax import lax
from jax.experimental import pallas as pl
from jax.experimental.pallas import tpu as pltpu

HEADS = 16
HEAD = 64
BLOCK = 64
RANDOM = 3
GLOBAL = 2
NEGATIVE = -1e30
GROUP = 4
WIDE = GROUP * HEAD
LISTED = 8 * BLOCK
CHUNK = 512
SCALING = HEAD ** (-0.5)


def dot_nt(left, right):
    return lax.dot_general(left, right, (((1,), (1,)), ((), ())), preferred_element_type=jnp.float32)


def dot_nn(left, right):
    return lax.dot_general(left, right, (((1,), (0,)), ((), ())), preferred_element_type=jnp.float32)


def dot_tn(left, right):
    return lax.dot_general(left, right, (((0,), (0,)), ((), ())), preferred_element_type=jnp.float32)


def spread_heads(rows, same_head):
    return jnp.concatenate([rows] * GROUP, 0) * same_head


def own_lanes(full):
    lane_head = lax.broadcasted_iota(jnp.int32, (BLOCK, WIDE), 1) // HEAD
    picked = full[:BLOCK]
    for head in range(1, GROUP):
        picked = jnp.where(lane_head == head, full[head * BLOCK : (head + 1) * BLOCK], picked)
    return picked


def rows_of(block):
    return pl.ds(pl.multiple_of(block * BLOCK, BLOCK), BLOCK)


def chosen(table_ref, row, first_head):
    base = (row * HEADS + first_head) * RANDOM
    return [[table_ref[base + head * RANDOM + pick] for head in range(GROUP)] for pick in range(RANDOM)]


def paired(ref, numbers, low_half, whole):
    parts = []
    for pair in range(GROUP // 2):
        lanes = slice(pair * 128, (pair + 1) * 128) if whole else slice(0, 128)
        first = ref[rows_of(numbers[2 * pair]), lanes]
        second = ref[rows_of(numbers[2 * pair + 1]), lanes]
        parts.append(jnp.where(low_half, first, second))
    return jnp.concatenate(parts, 1)


def listed_rows(ref, row, after, picks, low_half):
    parts = [ref[rows_of(row - 1), :], ref[rows_of(row), :], ref[rows_of(after), :]]
    parts += [paired(ref, numbers, low_half, True) for numbers in picks]
    parts.append(ref[: GLOBAL * BLOCK, :])
    return jnp.concatenate(parts, 0)


def listed_bias(bias_ref, row, picks, low_half):
    def twice(value):
        return jnp.concatenate([value] * (GROUP // 2), 1)

    parts = [twice(bias_ref[rows_of(row - 1), :]), twice(bias_ref[rows_of(row), :])]
    parts.append(twice(bias_ref[rows_of(row + 1), :]))
    parts += [paired(bias_ref, numbers, low_half, False) for numbers in picks]
    parts.append(twice(bias_ref[: GLOBAL * BLOCK, :]))
    return jnp.concatenate(parts, 0)


def lane_masks():
    low_half = lax.broadcasted_iota(jnp.int32, (BLOCK, 128), 1) < HEAD
    one = lax.broadcasted_iota(jnp.int32, (WIDE, WIDE), 0) // HEAD
    two = lax.broadcasted_iota(jnp.int32, (WIDE, WIDE), 1) // HEAD
    same_head = jnp.where(one == two, 1.0, 0.0).astype(jnp.bfloat16)
    return low_half, same_head


def forward_kernel(table_ref, q_ref, k_ref, v_ref, bias_ref, out_ref, lse_ref, score_ref):
    length = q_ref.shape[0]
    block_count = length // BLOCK
    first_head = pl.program_id(0) * GROUP
    low_half, same_head = lane_masks()

    def local_row(row, carried):
        picks = chosen(table_ref, row, first_head)
        after = jnp.minimum(row + 1, block_count - 1)
        query = spread_heads(q_ref[rows_of(row), :], same_head)
        keys = listed_rows(k_ref, row, after, picks, low_half)
        scores = dot_nt(keys, query) + listed_bias(bias_ref, row, picks, low_half)
        highest = jnp.max(scores, 0, keepdims=True)
        expanded = jnp.exp(scores - highest)
        total = jnp.sum(expanded, 0, keepdims=True)
        weights = (expanded * (1.0 / total)).astype(jnp.bfloat16)
        values = listed_rows(v_ref, row, after, picks, low_half)
        out_ref[rows_of(row), :] = own_lanes(dot_tn(weights, values)).astype(jnp.bfloat16)
        lse_ref[0, pl.ds(row, 1), :] = highest + jnp.log(total)
        return carried

    for row in range(GLOBAL):
        query = spread_heads(q_ref[row * BLOCK : (row + 1) * BLOCK, :], same_head)

        def score_chunk(chunk, highest):
            span = pl.ds(pl.multiple_of(chunk * CHUNK, CHUNK), CHUNK)
            bias = bias_ref[span, :]
            scores = dot_nt(k_ref[span, :], query) + jnp.concatenate([bias] * (GROUP // 2), 1)
            score_ref[span, :] = scores
            return jnp.maximum(highest, jnp.max(scores, 0, keepdims=True))

        highest = lax.fori_loop(
            0, length // CHUNK, score_chunk, jnp.full((1, WIDE), NEGATIVE, jnp.float32)
        )

        def total_chunk(chunk, total):
            span = pl.ds(pl.multiple_of(chunk * CHUNK, CHUNK), CHUNK)
            expanded = jnp.exp(score_ref[span, :] - highest)
            score_ref[span, :] = expanded
            return total + jnp.sum(expanded, 0, keepdims=True)

        total = lax.fori_loop(
            0, length // CHUNK, total_chunk, jnp.zeros((1, WIDE), jnp.float32)
        )
        inverse = 1.0 / total

        def mix_chunk(chunk, mixed):
            span = pl.ds(pl.multiple_of(chunk * CHUNK, CHUNK), CHUNK)
            weights = (score_ref[span, :] * inverse).astype(jnp.bfloat16)
            return mixed + own_lanes(dot_tn(weights, v_ref[span, :]))

        mixed = lax.fori_loop(
            0, length // CHUNK, mix_chunk, jnp.zeros((BLOCK, WIDE), jnp.float32)
        )
        out_ref[row * BLOCK : (row + 1) * BLOCK, :] = mixed.astype(jnp.bfloat16)
        lse_ref[0, row : row + 1, :] = highest + jnp.log(total)

    lax.fori_loop(GLOBAL, block_count, local_row, 0)


def backward_kernel(
    table_ref,
    q_ref,
    k_ref,
    v_ref,
    grad_ref,
    bias_ref,
    lse_ref,
    *refs,
    first_group,
):
    dq_ref, dk_ref, dv_ref, chance_ref, pull_ref, dk_sum, dv_sum = refs[-7:]
    length = q_ref.shape[0]
    block_count = length // BLOCK
    first_head = (pl.program_id(0) + first_group) * GROUP

    low_half, same_head = lane_masks()

    for row in range(GLOBAL):
        query = spread_heads(q_ref[row * BLOCK : (row + 1) * BLOCK, :], same_head)
        grad = spread_heads(grad_ref[row * BLOCK : (row + 1) * BLOCK, :], same_head)
        lse = lse_ref[0, row : row + 1, :]

        def chance_chunk(chunk, centred):
            span = pl.ds(pl.multiple_of(chunk * CHUNK, CHUNK), CHUNK)
            bias = bias_ref[span, :]
            scores = dot_nt(k_ref[span, :], query) + jnp.concatenate([bias] * (GROUP // 2), 1)
            chances = jnp.exp(scores - lse)
            pulls = dot_nt(v_ref[span, :], grad)
            chance_ref[span, :] = chances
            pull_ref[span, :] = pulls
            return centred + jnp.sum(chances * pulls, 0, keepdims=True)

        centred = lax.fori_loop(
            0, length // CHUNK, chance_chunk, jnp.zeros((1, WIDE), jnp.float32)
        )

        def grad_chunk(chunk, query_grad):
            span = pl.ds(pl.multiple_of(chunk * CHUNK, CHUNK), CHUNK)
            chances = chance_ref[span, :]
            score_grad = (chances * (pull_ref[span, :] - centred)).astype(jnp.bfloat16)
            key_part = dot_nn(score_grad, query)
            value_part = dot_nn(chances.astype(jnp.bfloat16), grad)
            if row == 0:
                dk_sum[span, :] = key_part
                dv_sum[span, :] = value_part
            else:
                dk_sum[span, :] += key_part
                dv_sum[span, :] += value_part
            return query_grad + own_lanes(dot_tn(score_grad, k_ref[span, :]))

        query_grad = lax.fori_loop(
            0, length // CHUNK, grad_chunk, jnp.zeros((BLOCK, WIDE), jnp.float32)
        )
        dq_ref[row * BLOCK : (row + 1) * BLOCK, :] = (query_grad * SCALING).astype(jnp.bfloat16)

    dk_sum[length : length + BLOCK, :] = jnp.zeros((BLOCK, WIDE), jnp.float32)
    dv_sum[length : length + BLOCK, :] = jnp.zeros((BLOCK, WIDE), jnp.float32)

    def add_rows(sum_ref, part, row, picks):
        near = pl.ds(pl.multiple_of((row - 1) * BLOCK, BLOCK), 3 * BLOCK)
        sum_ref[near, :] += part[: 3 * BLOCK]
        for pick, numbers in enumerate(picks):
            piece = part[(3 + pick) * BLOCK : (4 + pick) * BLOCK]
            for head, number in enumerate(numbers):
                lanes = slice(head // 2 * 128, (head // 2 + 1) * 128)
                mine = low_half if head % 2 == 0 else jnp.logical_not(low_half)
                sum_ref[rows_of(number), lanes] += jnp.where(mine, piece[:, lanes], 0.0)
        sum_ref[: GLOBAL * BLOCK, :] += part[6 * BLOCK :]

    def local_row(row, carried):
        picks = chosen(table_ref, row, first_head)
        after = jnp.minimum(row + 1, block_count - 1)
        query = spread_heads(q_ref[rows_of(row), :], same_head)
        grad = spread_heads(grad_ref[rows_of(row), :], same_head)
        keys = listed_rows(k_ref, row, after, picks, low_half)
        values = listed_rows(v_ref, row, after, picks, low_half)
        scores = dot_nt(keys, query) + listed_bias(bias_ref, row, picks, low_half)
        chances = jnp.exp(scores - lse_ref[0, pl.ds(row, 1), :])
        pulls = dot_nt(values, grad)
        centred = jnp.sum(chances * pulls, 0, keepdims=True)
        score_grad = (chances * (pulls - centred)).astype(jnp.bfloat16)
        query_grad = own_lanes(dot_tn(score_grad, keys))
        dq_ref[rows_of(row), :] = (query_grad * SCALING).astype(jnp.bfloat16)
        add_rows(dk_sum, dot_nn(score_grad, query), row, picks)
        add_rows(dv_sum, dot_nn(chances.astype(jnp.bfloat16), grad), row, picks)
        return carried

    lax.fori_loop(GLOBAL, block_count, local_row, 0)
    dk_ref[...] = dk_sum[:length, :].astype(jnp.bfloat16)
    dv_ref[...] = dv_sum[:length, :].astype(jnp.bfloat16)


def attention_specs(length, count):
    rows = pl.BlockSpec((length, WIDE), lambda group, table: (0, group))
    bias = pl.BlockSpec((length + BLOCK, 128), lambda group, table: (0, 0))
    lse = pl.BlockSpec((1, length // BLOCK, WIDE), lambda group, table: (group, 0, 0))
    return [rows] * count, bias, lse


def live_bias(live_keys):
    padded = jnp.concatenate([live_keys, jnp.zeros((BLOCK,), jnp.bool_)])
    return jnp.broadcast_to(jnp.where(padded, 0.0, NEGATIVE)[:, None], (padded.shape[0], 128))


def attention_forward(queries, key_rows, value_rows, bias, table):
    length, width = queries.shape
    rows, bias_spec, lse_spec = attention_specs(length, 3)
    units = width // WIDE * (length // BLOCK + 6)
    return pl.pallas_call(
        forward_kernel,
        grid_spec=pltpu.PrefetchScalarGridSpec(
            num_scalar_prefetch=1,
            grid=(width // WIDE,),
            in_specs=rows + [bias_spec],
            out_specs=[rows[0], lse_spec],
            scratch_shapes=[pltpu.VMEM((length, WIDE), jnp.float32)],
        ),
        out_shape=[
            jax.ShapeDtypeStruct((length, width), jnp.bfloat16),
            jax.ShapeDtypeStruct((width // WIDE, length // BLOCK, WIDE), jnp.float32),
        ],
        cost_estimate=pl.CostEstimate(
            flops=units * 4 * LISTED * WIDE * WIDE,
            bytes_accessed=8 * length * width,
            transcendentals=units * LISTED * WIDE,
        ),
        compiler_params=pltpu.CompilerParams(vmem_limit_bytes=48 << 20),
        name="block_attention",
    )(table, queries, key_rows, value_rows, bias)


def attention_backward(operands, table, bias, lse, first_group, groups, earlier):
    length, width = operands[0].shape
    rows = pl.BlockSpec((length, WIDE), lambda group, table: (0, group + first_group))
    bias_spec = pl.BlockSpec((length + BLOCK, 128), lambda group, table: (0, 0))
    lse_spec = pl.BlockSpec(
        (1, length // BLOCK, WIDE), lambda group, table: (group + first_group, 0, 0)
    )
    units = groups * (length // BLOCK + 6)
    return pl.pallas_call(
        functools.partial(backward_kernel, first_group=first_group),
        grid_spec=pltpu.PrefetchScalarGridSpec(
            num_scalar_prefetch=1,
            grid=(groups,),
            in_specs=[rows] * 4
            + [bias_spec, lse_spec]
            + [pl.BlockSpec(memory_space=pl.ANY)] * len(earlier),
            out_specs=[rows] * 3,
            scratch_shapes=[
                pltpu.VMEM((length, WIDE), jnp.float32),
                pltpu.VMEM((length, WIDE), jnp.float32),
                pltpu.VMEM((length + BLOCK, WIDE), jnp.float32),
                pltpu.VMEM((length + BLOCK, WIDE), jnp.float32),
            ],
        ),
        out_shape=[jax.ShapeDtypeStruct((length, width), jnp.bfloat16)] * 3,
        input_output_aliases={7 + number: number for number in range(len(earlier))},
        cost_estimate=pl.CostEstimate(
            flops=units * 10 * LISTED * WIDE * WIDE,
            bytes_accessed=14 * length * WIDE * groups,
            transcendentals=units * LISTED * WIDE,
        ),
        compiler_params=pltpu.CompilerParams(vmem_limit_bytes=56 << 20),
        name="block_attention_grad",
    )(table, *operands, bias, lse, *earlier)


TILE = 256
SLAB = 512
EPSILON = 1e-05
GELU_SCALE = 0.7978845608028654
GELU_CUBE = 0.044715


def centred_rows(values_in):
    centre = values_in - jnp.mean(values_in, -1, keepdims=True)
    inverse = lax.rsqrt(jnp.mean(centre * centre, -1, keepdims=True) + EPSILON)
    return centre * inverse, inverse


def norm_back(grad_rows, unit_rows, inverse, norm_gain):
    scaled = grad_rows * norm_gain
    adjusted = (
        scaled
        - jnp.mean(scaled, -1, keepdims=True)
        - unit_rows * jnp.mean(scaled * unit_rows, -1, keepdims=True)
    )
    return adjusted * inverse


def project_kernel(
    token_ref, wq_ref, wk_ref, wv_ref, vector_ref, normed_ref, q_ref, k_ref, v_ref
):
    unit_rows, _ = centred_rows(token_ref[...].astype(jnp.float32))
    normed = (unit_rows * vector_ref[0:1, :] + vector_ref[1:2, :]).astype(jnp.bfloat16)
    normed_ref[...] = normed
    q_ref[...] = ((dot_nn(normed, wq_ref[...]) + vector_ref[2:3, :]) * SCALING).astype(jnp.bfloat16)
    k_ref[...] = dot_nn(normed, wk_ref[...]).astype(jnp.bfloat16)
    v_ref[...] = (dot_nn(normed, wv_ref[...]) + vector_ref[3:4, :]).astype(jnp.bfloat16)


def dense_kernel(
    token_ref,
    mixture_ref,
    wo_ref,
    wi_ref,
    vector_ref,
    bias_ref,
    residual_ref,
    normed_ref,
    active_ref,
    slope_ref,
):
    branch = dot_nn(mixture_ref[...], wo_ref[...]) + vector_ref[4:5, :]
    residual = token_ref[...].astype(jnp.float32) + branch
    residual_ref[...] = residual
    unit_rows, _ = centred_rows(residual)
    normed = (unit_rows * vector_ref[5:6, :] + vector_ref[6:7, :]).astype(jnp.bfloat16)
    normed_ref[...] = normed
    for start in range(0, wi_ref.shape[1], SLAB):
        lanes = slice(start, start + SLAB)
        hidden = dot_nn(normed, wi_ref[:, lanes]) + bias_ref[:, lanes]
        square = hidden * hidden
        bend = jnp.tanh(GELU_SCALE * hidden * (1.0 + GELU_CUBE * square))
        half = 0.5 + 0.5 * bend
        active_ref[:, lanes] = (hidden * half).astype(jnp.bfloat16)
        inner = GELU_SCALE + (3.0 * GELU_SCALE * GELU_CUBE) * square
        slope = half + 0.5 * hidden * (1.0 - bend * bend) * inner
        slope_ref[:, lanes] = slope.astype(jnp.bfloat16)


def add_sums(sum_ref, columns):
    rows = [jnp.sum(column.astype(jnp.float32), 0, keepdims=True) for column in columns]

    @pl.when(pl.program_id(0) == 0)
    def _():
        sum_ref[...] = jnp.zeros_like(sum_ref)

    for place, row in enumerate(rows):
        sum_ref[place : place + 1, :] += row


def dense_grad_kernel(
    cot_ref,
    slope_ref,
    residual_ref,
    wu_ref,
    wi_ref,
    wo_ref,
    vector_ref,
    hidden_ref,
    residual_grad_ref,
    branch_ref,
    mixture_ref,
    sum_ref,
    bias_ref,
):
    cot = cot_ref[...]

    @pl.when(pl.program_id(0) == 0)
    def _():
        bias_ref[...] = jnp.zeros_like(bias_ref)

    normed_grad = jnp.zeros(cot.shape, jnp.float32)
    for start in range(0, wi_ref.shape[1], SLAB):
        lanes = slice(start, start + SLAB)
        active_grad = dot_nt(cot, wu_ref[lanes, :])
        hidden = (active_grad * slope_ref[:, lanes].astype(jnp.float32)).astype(jnp.bfloat16)
        hidden_ref[:, lanes] = hidden
        bias_ref[0:1, lanes] += jnp.sum(hidden.astype(jnp.float32), 0, keepdims=True)
        normed_grad += dot_nt(hidden, wi_ref[:, lanes])
    unit_rows, inverse = centred_rows(residual_ref[...])
    residual_grad = cot.astype(jnp.float32) + norm_back(
        normed_grad, unit_rows, inverse, vector_ref[5:6, :]
    )
    residual_grad_ref[...] = residual_grad
    branch = residual_grad.astype(jnp.bfloat16)
    branch_ref[...] = branch
    mixture_ref[...] = dot_nt(branch, wo_ref[...]).astype(jnp.bfloat16)
    add_sums(sum_ref, [normed_grad * unit_rows, normed_grad, cot, branch])


def project_grad_kernel(
    token_ref,
    residual_grad_ref,
    dq_ref,
    dk_ref,
    dv_ref,
    wq_ref,
    wk_ref,
    wv_ref,
    vector_ref,
    input_ref,
    sum_ref,
):
    normed_grad = dot_nt(dq_ref[...], wq_ref[...])
    normed_grad += dot_nt(dk_ref[...], wk_ref[...])
    normed_grad += dot_nt(dv_ref[...], wv_ref[...])
    unit_rows, inverse = centred_rows(token_ref[...].astype(jnp.float32))
    input_ref[...] = residual_grad_ref[...] + norm_back(
        normed_grad, unit_rows, inverse, vector_ref[0:1, :]
    )
    add_sums(sum_ref, [normed_grad * unit_rows, normed_grad, dq_ref[...], dv_ref[...]])


def output_kernel(residual_ref, active_ref, wu_ref, vector_ref, out_ref):
    added = dot_nn(active_ref[...], wu_ref[...]) + vector_ref[7:8, :]
    out_ref[...] = (residual_ref[...] + added).astype(jnp.bfloat16)


def row_call(kernel, name, moving, fixed, outs, flops):
    length = moving[0].shape[0]

    def tiled(width):
        return pl.BlockSpec((TILE, width), lambda tile: (tile, 0))

    def whole(shape, **mode):
        return pl.BlockSpec(shape, lambda tile: (0, 0), **mode)

    out_specs, out_shape = [], []
    for rows, width, kind in outs:
        out_specs.append(tiled(width) if rows is None else whole((rows, width)))
        out_shape.append(jax.ShapeDtypeStruct((rows or length, width), kind))
    size = sum(value.size * value.dtype.itemsize for value in list(moving) + list(fixed))
    size += sum(value.size * value.dtype.itemsize for value in out_shape)
    return pl.pallas_call(
        kernel,
        grid=(length // TILE,),
        in_specs=[tiled(value.shape[1]) for value in moving]
        + [whole(value.shape, pipeline_mode=pl.Buffered(1)) for value in fixed],
        out_specs=out_specs,
        out_shape=out_shape,
        cost_estimate=pl.CostEstimate(flops=flops, bytes_accessed=size, transcendentals=0),
        compiler_params=pltpu.CompilerParams(vmem_limit_bytes=56 << 20),
        name=name,
    )(*moving, *fixed)


from jax.sharding import PartitionSpec as P

SPLIT = ("dp", "fsdp")


def across_rows(left, right):
    return jnp.einsum("ti,tj->ij", left, right, preferred_element_type=jnp.float32)


class Devices:
    def __init__(self, mesh):
        self.inner = mesh.shape["fsdp"]
        self.count = mesh.shape["dp"] * self.inner
        self.bits = self.count.bit_length() - 1
        chip = self.inner.bit_length() - 1
        others = [bit for bit in range(self.bits) if bit != chip]
        plane = [others.pop(0), others.pop()]
        line = [others[start : start + 2] for start in range(0, len(others), 2)]
        self.flat = [[chip], plane] + line
        self.tall = [[chip]] + line + [plane]
        self.chip, self.plane, self.line = chip, plane, others

    def here(self):
        return lax.axis_index("dp") * self.inner + lax.axis_index("fsdp")

    def swap(self, value, mask):
        return lax.ppermute(value, SPLIT, [(place, place ^ mask) for place in range(self.count)])

    def turned(self, turn):
        ring = self.line[::-1] + self.plane
        turn = turn % len(ring)
        return ring[turn:] + ring[:turn] + [self.chip]

    def gather(self, shard, turn, steps=None, before=None):
        whole = shard if before is None else before[0]
        have = [] if before is None else list(before[1])
        for bit in self.turned(turn)[len(have) :][:steps]:
            taken = self.swap(whole, 1 << bit)
            dim = sum(1 for other in have if other > bit)
            have.append(bit)
            first = (self.here() >> bit) & 1 == 0
            whole = jnp.where(
                first, jnp.stack([whole, taken], dim), jnp.stack([taken, whole], dim)
            )
        if steps is not None:
            return whole, have
        return whole.reshape((-1,) + shard.shape[1:])


class Halving:
    def __init__(self, devices, part, stages):
        self.devices = devices
        rounded = part.astype(jnp.bfloat16)
        self.total = rounded.reshape((2,) * devices.bits + (-1,) + part.shape[1:])
        self.left = list(range(devices.bits))[::-1]
        self.stages = list(stages)

    def pick(self, mask, stage):
        value = self.total
        dims = [self.left.index(bit) for bit in stage]
        for dim, bit in sorted(zip(dims, stage), reverse=True):
            wanted = ((self.devices.here() ^ mask) >> bit) & 1
            value = lax.dynamic_index_in_dim(value, wanted, dim, keepdims=False)
        return value

    def masks(self):
        found = [0]
        for bit in self.stages[0]:
            found += [mask | 1 << bit for mask in found]
        return found[1:]

    def given(self):
        return [self.pick(mask, self.stages[0]).astype(jnp.bfloat16) for mask in self.masks()]

    def move(self, given):
        self.taken = [
            self.devices.swap(value, mask) for value, mask in zip(given, self.masks())
        ]

    def land(self):
        kept = self.pick(0, self.stages[0]).astype(jnp.float32)
        for value in self.taken:
            kept = kept + value.astype(jnp.float32)
        self.left = [bit for bit in self.left if bit not in self.stages[0]]
        self.total = kept
        self.stages.pop(0)


class Whole:
    def __init__(self, devices, part, stages):
        self.devices, self.total, self.stages = devices, part, list(stages)

    masks = Halving.masks
    move = Halving.move

    def given(self):
        return [self.total] * len(self.masks())

    def land(self):
        for value in self.taken:
            self.total = self.total + value
        self.stages.pop(0)


def launch(sums, value):
    given = [item.given() for item in sums]
    given, value = lax.optimization_barrier((given, value))
    for item, parts in zip(sums, given):
        item.move(parts)
    return value


def solution(mesh):
    devices = Devices(mesh)

    def body(
        tokens,
        cotangent,
        doc_lengths,
        key_keep,
        random_blocks,
        attention_gain,
        attention_shift,
        w_query,
        b_query,
        w_key,
        w_value,
        b_value,
        w_output,
        b_output,
        dense_gain,
        dense_shift,
        w_inner,
        b_inner,
        w_outer,
        b_outer,
    ):
        length, width = tokens.shape
        share = attention_gain.shape[0]
        vectors = (
            attention_gain,
            attention_shift,
            b_query,
            b_value,
            b_output,
            dense_gain,
            dense_shift,
            b_outer,
            b_inner,
        )
        begun = [
            devices.gather(shard, turn, 1) for turn, shard in enumerate((w_query, w_key, w_value))
        ]
        begun, vectors = lax.optimization_barrier(([value[0] for value in begun], vectors))
        w_query, w_key, w_value = [
            devices.gather(shard, turn, None, (value, devices.turned(turn)[:1]))
            for turn, (shard, value) in enumerate(zip((w_query, w_key, w_value), begun))
        ]
        joined = devices.gather(jnp.concatenate(vectors)[None, :], 0).astype(jnp.float32)
        vector_rows = (
            joined[:, : 8 * share].reshape(-1, 8, share).transpose(1, 0, 2).reshape(8, width)
        )
        inner_bias = joined[:, 8 * share :].reshape(1, -1)
        w_output = lax.all_gather(w_output, SPLIT, axis=0, tiled=True)
        w_inner = lax.all_gather(w_inner, SPLIT, axis=0, tiled=True)
        w_outer = lax.all_gather(w_outer, SPLIT, axis=0, tiled=True)

        places = jnp.arange(length, dtype=jnp.int32)
        live_keys = (key_keep > 0) & (places < doc_lengths[0]) | (places == 0)
        bias = live_bias(live_keys)
        table = random_blocks.reshape(-1)
        hidden_width = w_inner.shape[1]
        square = 2 * length * width * width
        low, high = jnp.bfloat16, jnp.float32
        normed, queries, key_rows, value_rows = row_call(
            project_kernel,
            "project",
            (tokens,),
            (w_query, w_key, w_value, vector_rows),
            [(None, width, low)] * 4,
            3 * square,
        )
        mixture, lse = attention_forward(queries, key_rows, value_rows, bias, table)
        residual, dense_low, active, slope = row_call(
            dense_kernel,
            "dense",
            (tokens, mixture),
            (w_output, w_inner, vector_rows, inner_bias),
            [(None, width, high), (None, width, low)] + [(None, hidden_width, low)] * 2,
            5 * square,
        )

        outer_sum = Halving(devices, across_rows(active, cotangent), devices.flat)
        slope = launch([outer_sum], slope)
        hidden_grad, residual_grad, branch_grad, mixture_grad, dense_sums, inner_sums = row_call(
            dense_grad_kernel,
            "dense_grad",
            (cotangent, slope, residual),
            (w_outer, w_inner, w_output, vector_rows),
            [(None, hidden_width, low), (None, width, high), (None, width, low)]
            + [(None, width, low), (8, width, high), (8, hidden_width, high)],
            9 * square,
        )
        outer_sum.land()
        hidden_grad = launch([outer_sum], hidden_grad)
        inner_sum = Halving(devices, across_rows(dense_low, hidden_grad), devices.flat)
        mixture_grad = launch([inner_sum], mixture_grad)
        operands = [queries, key_rows, value_rows, mixture_grad]
        grads = attention_backward(operands, table, bias, lse, 0, 1, ())
        outer_sum.land()
        inner_sum.land()
        output_sum = Halving(devices, across_rows(mixture, branch_grad), devices.flat)
        operands, grads = launch([outer_sum, inner_sum, output_sum], (operands, grads))
        grads = attention_backward(operands, table, bias, lse, 1, 2, grads)
        outer_sum.land()
        inner_sum.land()
        output_sum.land()
        operands, grads = launch([inner_sum, output_sum], (operands, grads))
        query_low, key_low, value_low = attention_backward(
            operands, table, bias, lse, 3, 1, grads
        )
        inner_sum.land()
        output_sum.land()
        query_low = launch([output_sum], query_low)
        near = [
            Halving(devices, across_rows(normed, query_low), devices.flat),
            Halving(devices, across_rows(normed, key_low), devices.flat),
            Halving(devices, across_rows(normed, value_low), devices.tall),
        ]
        output_sum.land()
        residual_grad = launch(near, residual_grad)
        input_grad, project_sums = row_call(
            project_grad_kernel,
            "project_grad",
            (tokens, residual_grad, query_low, key_low, value_low),
            (w_query, w_key, w_value, vector_rows),
            [(None, width, high), (8, width, high)],
            3 * square,
        )
        for item in near:
            item.land()
        packed = jnp.concatenate(
            [project_sums[:4], dense_sums[:4], inner_sums[:1].reshape(-1, width)], 0
        )
        vector_sum = Whole(devices, packed, devices.flat)
        active = launch(near + [vector_sum], active)
        (layer_output,) = row_call(
            output_kernel,
            "output",
            (residual, active),
            (w_outer, vector_rows),
            [(None, width, low)],
            4 * square,
        )
        for item in near + [vector_sum]:
            item.land()
        everything = near + [vector_sum, outer_sum, inner_sum, output_sum]
        while any(item.stages for item in everything):
            waiting = [item for item in everything if item.stages]
            for item in waiting:
                item.move(item.given())
            for item in waiting:
                item.land()

        here = devices.here()
        sums = lax.dynamic_slice(vector_sum.total[:8], (0, here * share), (8, share))
        wide = share * hidden_width // width
        inner_bias_grad = lax.dynamic_slice(vector_sum.total[8:].reshape(-1), (here * wide,), (wide,))

        def shard(item, like):
            return item.total.reshape(like.shape[0] // devices.count, like.shape[1])

        return (
            layer_output,
            input_grad,
            sums[0],
            sums[1],
            shard(near[0], w_query),
            sums[2],
            shard(near[1], w_key),
            shard(near[2], w_value),
            sums[3],
            shard(output_sum, w_output),
            sums[7],
            sums[4],
            sums[5],
            shard(inner_sum, w_inner),
            inner_bias_grad,
            shard(outer_sum, w_outer),
            sums[6],
        )

    rows = P(SPLIT, None)
    flat = P(SPLIT)
    return jax.shard_map(
        body,
        mesh=mesh,
        in_specs=(
            (rows, rows, flat, flat, P(SPLIT, None, None), flat, flat, rows, flat, rows, rows)
            + (flat, rows, flat, flat, flat, rows, flat, rows, flat)
        ),
        out_specs=(
            (rows, rows, flat, flat, rows, flat, rows, rows, flat, rows, flat, flat, flat)
            + (rows, flat, rows, flat)
        ),
        check_vma=False,
    )
```
